512 devices in a mesh: member: 64 (over z, y), space: 8 (over x, core).
Axes of the slice: x: 4, y: 8, z: 8, core: 2. Of those that a mesh axis runs over, the one named last changes fastest.
Arguments:
- prior_field: bfloat16 [64, 4096, 8, 128], P('member', 'space'), may hold values from -6 to 6
- replica_predicted_readings: float32 [64, 4096, 128], P('member', 'space'), may hold values from -6 to 6
- replica_reading_noise: float32 [64, 4096, 128], P('member', 'space'), may hold values from -12 to 12
- sensor_readings: float32 [4096, 128], P('space'), may hold values from -6 to 6
- reading_noise_power: float32 [4096, 128], P('space'), may hold values from 2 to 8
- sensor_patch_tally: int32 [4096], P('space'), may hold values from 1 to 128
- sensor_patch_start: int32 [4096], replicated, may hold values from 0 to 63, as said below
- neighbour_listing: int32 [4096, 8], P('space'), may hold values from 0 to 4095, as said below
Outputs:
- increment: bfloat16 [64, 4096, 8, 128], P('member', 'space')
The draws below stay inside these ranges and needn't reach their ends.
Inputs may be any that keep to these rules, and one draw needn't show every extreme that they name: `neighbour_listing`: every row lists 8 different observation blocks, each in a tile whose two tile indices differ from those of the state block's tile by at most one. `sensor_patch_start`: the coordinate of an observation block in tile (p, q) lies from p * 8 to p * 8 + 7.
All inputs are finite; a program needn't handle non-finite values.
Results may differ from the reference program's by a relative error of at most 0.001.
Values may be sent and summed in bfloat16 or wider, within the bound.
A program may use at most 64 MiB of HBM per device.

```python
import math
import jax
import jax.numpy as jnp
from jax import lax

PATCH_CAPACITY = 128
STRATA_NUMBER = 8
NNB = 8
PATCHES_PER_AREA = 8
OB_DEV = 8
REPLICA_NUMBER = 64
MODEL_PATCHES = 4096
SENSOR_PATCHES = 4096
N_MEMBER = 64
N_SPACE = 8


def draw_neighbour_listing(key, part):
    blocks = jnp.arange(MODEL_PATCHES, dtype=jnp.int32)
    tile_x = blocks // (PATCHES_PER_AREA * N_MEMBER)
    tile_y = blocks // PATCHES_PER_AREA % N_MEMBER
    offsets = jnp.arange(9 * OB_DEV, dtype=jnp.int32)
    shift_y = offsets // (3 * OB_DEV) - 1
    shift_x = offsets // OB_DEV % 3 - 1
    within = offsets % OB_DEV
    candidate_y = tile_y[:, None] + shift_y[None, :]
    candidate_x = tile_x[:, None] + shift_x[None, :]
    valid = (candidate_y >= 0) & (candidate_y < N_MEMBER) & (candidate_x >= 0) & (candidate_x < N_SPACE)
    identity = (candidate_x * N_MEMBER + candidate_y) * OB_DEV + within[None, :]
    scores = jax.random.randint(key, (MODEL_PATCHES, 9 * OB_DEV), 0, 4096) * (9 * OB_DEV) + offsets[None, :]
    scores = jnp.where(valid, scores, -1)
    ranked, picks = lax.top_k(scores, NNB)
    return jnp.take_along_axis(identity, picks, axis=1).astype(jnp.int32)


def draw_sensor_patch_start(key, part):
    blocks = jnp.arange(SENSOR_PATCHES, dtype=jnp.int32)
    tile_x = blocks // (OB_DEV * N_MEMBER)
    return (tile_x * PATCHES_PER_AREA + jax.random.randint(key, (SENSOR_PATCHES,), 0, PATCHES_PER_AREA)).astype(jnp.int32)


def draw_sensor_patch_tally(key, part):
    first = jax.random.randint(jax.random.fold_in(key, 11), (SENSOR_PATCHES,), 1, PATCH_CAPACITY + 1)
    second = jax.random.randint(jax.random.fold_in(key, 12), (SENSOR_PATCHES,), 1, PATCH_CAPACITY + 1)
    counts = jnp.minimum(first, second)
    blocks = jnp.arange(SENSOR_PATCHES, dtype=jnp.int32)
    counts = jnp.where(blocks == 0, PATCH_CAPACITY, counts)
    counts = jnp.where(blocks == 1, 1, counts)
    return counts.astype(jnp.int32)


def shard_levels(stream_key, extent, split, least, top_value):
    factor_of, own = 1.0, jax.random.fold_in(stream_key, 6)
    for position, blocks in split:
        steps = jnp.exp(jax.random.uniform(jax.random.fold_in(own, position), (blocks,), jnp.float32, least / len(split), top_value / len(split)))
        factor_of = factor_of * jnp.repeat(steps, extent[position] // blocks).reshape([-1 if axis == position else 1 for axis in range(len(extent))])
    return factor_of


def normal_values(key, extent, spread, bound, shards=(), held_as=jnp.bfloat16):
    values = jax.random.normal(key, extent, jnp.float32) * spread
    if len(shards) > 0:
        values = shard_levels(key, extent, shards, -0.22, 0.18) * values
    return jnp.clip(values, min=-bound, max=bound).astype(held_as)


def setup_inputs(seed: int = 0) -> dict:
    splits = jax.random.split(jax.random.key(seed), 9)
    return {
        "prior_field": normal_values(splits[0], (REPLICA_NUMBER, MODEL_PATCHES, STRATA_NUMBER, PATCH_CAPACITY), 1.0, 6.0, ((0, 64), (1, 8))),
        "replica_predicted_readings": normal_values(splits[1], (REPLICA_NUMBER, SENSOR_PATCHES, PATCH_CAPACITY), 1.0, 6.0, ((0, 64), (1, 8)), jnp.float32),
        "replica_reading_noise": normal_values(splits[2], (REPLICA_NUMBER, SENSOR_PATCHES, PATCH_CAPACITY), 2.0, 12.0, ((0, 64), (1, 8)), jnp.float32),
        "sensor_readings": normal_values(splits[3], (SENSOR_PATCHES, PATCH_CAPACITY), 1.0, 6.0, ((0, 8),), jnp.float32),
        "reading_noise_power": jnp.clip(jnp.exp(math.log(8.0) - 1.3862944 * jax.random.uniform(splits[4], (SENSOR_PATCHES, PATCH_CAPACITY), jnp.float32) ** shard_levels(splits[4], (SENSOR_PATCHES, PATCH_CAPACITY), ((0, 8),), -0.2, 0.2)), 2.0, 8.0),
        "sensor_patch_tally": draw_sensor_patch_tally(jax.random.fold_in(splits[8], 71), 0),
        "sensor_patch_start": draw_sensor_patch_start(jax.random.fold_in(splits[8], 71), 0),
        "neighbour_listing": draw_neighbour_listing(jax.random.fold_in(splits[8], 71), 0),
    }


def reference(prior_field, replica_predicted_readings, replica_reading_noise, sensor_readings, reading_noise_power, sensor_patch_tally, sensor_patch_start, neighbour_listing):
    replica_fields = prior_field.shape[0]
    highest = lax.Precision.HIGHEST
    prior_average = jnp.mean(replica_predicted_readings, axis=0)
    prior_deviation = replica_predicted_readings - prior_average[None]
    dispersion = jnp.sum(prior_deviation * prior_deviation, axis=0) / (replica_fields - 1)
    slots = jnp.arange(PATCH_CAPACITY, dtype=jnp.int32)
    active_mask = (slots[None, :] < sensor_patch_tally[:, None]).astype(jnp.float32)
    gain_factors = active_mask[None] * (sensor_readings[None] + replica_reading_noise - replica_predicted_readings) / (dispersion + reading_noise_power)[None]
    products = jnp.einsum("mbj,nbj->bmn", prior_deviation, gain_factors, precision=highest)
    blocks = jnp.arange(MODEL_PATCHES, dtype=jnp.int32)
    tile_x = blocks // (PATCHES_PER_AREA * N_MEMBER)
    tile_y = (blocks // PATCHES_PER_AREA) % N_MEMBER
    state_x = tile_x * PATCHES_PER_AREA + blocks % PATCHES_PER_AREA
    target_y = (neighbour_listing // OB_DEV) % N_MEMBER
    target_x = sensor_patch_start[neighbour_listing]
    delta_x = (state_x[:, None] - target_x).astype(jnp.float32)
    delta_y = (tile_y[:, None] - target_y).astype(jnp.float32)
    distance = delta_x * delta_x + delta_y * delta_y
    taper = 1.0 / (1.0 + distance / float(PATCHES_PER_AREA * PATCHES_PER_AREA))
    mixing = jnp.zeros((MODEL_PATCHES, replica_fields, replica_fields), jnp.float32)
    for column in range(NNB):
        mixing = mixing + taper[:, column, None, None] * products[neighbour_listing[:, column]]
    mixing = mixing / (replica_fields - 1)

    def one_group(group, output):
        starting_shift = (group * PATCHES_PER_AREA).astype(jnp.int32)
        numeric_items = lax.dynamic_slice_in_dim(prior_field, starting_shift, PATCHES_PER_AREA, 1).astype(jnp.float32)
        anomaly = numeric_items - jnp.mean(numeric_items, axis=0, keepdims=True)
        local_mix = lax.dynamic_slice_in_dim(mixing, starting_shift, PATCHES_PER_AREA, 0)
        result = jnp.einsum("mslc,smn->nslc", anomaly, local_mix, precision=highest).astype(jnp.bfloat16)
        return lax.dynamic_update_slice_in_dim(output, result, starting_shift, 1)

    output = jnp.zeros((replica_fields, MODEL_PATCHES, STRATA_NUMBER, PATCH_CAPACITY), jnp.bfloat16)
    return lax.fori_loop(0, MODEL_PATCHES // PATCHES_PER_AREA, one_group, output)
```

```python
import jax
import jax.numpy as jnp
from jax import lax
from jax.experimental import pallas as pl
from jax.experimental.pallas import tpu as pltpu
from jax.sharding import PartitionSpec as P

MESH = pl.DeviceIdType.MESH
SIDE = 8
MEMBERS = 64
STRIPS = 8
BLOCKS = 8
LEVELS = 8
CELLS = 128
CHUNK = 4
F32 = jnp.float32
BF16 = jnp.bfloat16


def far_first():
    def span(a):
        return min(a, SIDE - a)

    def rank(offset):
        a, b = span(offset[0]), span(offset[1])
        return (-(a + b), -max(a, b), min(offset))

    offsets = [(a, b) for a in range(SIDE) for b in range(SIDE) if (a, b) != (0, 0)]
    return sorted(offsets, key=rank)


OFFSETS = far_first()


def kernel(
    prior,
    model,
    noise,
    sensor,
    power,
    tally,
    select,
    out,
    got_model,
    got_noise,
    got_prior,
    mine_sensor,
    mine_power,
    products,
    partial,
    got_partial,
    mixing,
    wide_in,
    wide_out,
    increment,
    send_sems,
    recv_sems,
    local_sems,
    strip_sems,
    line_sems,
):
    me = lax.axis_index("member")
    strip = lax.axis_index("space")
    row, column = me // SIDE, lax.rem(me, SIDE)

    def member(offset):
        return lax.rem(row + offset[0], SIDE) * SIDE + lax.rem(column + offset[1], SIDE)

    peers = [member(offset) for offset in OFFSETS]
    east, west = lax.rem(strip + 1, STRIPS), lax.rem(strip + STRIPS - 1, STRIPS)
    north, south = lax.rem(me + 1, MEMBERS), lax.rem(me + MEMBERS - 1, MEMBERS)

    own = [
        pltpu.make_async_copy(
            sensor.at[pl.ds(me * BLOCKS, BLOCKS)], mine_sensor, local_sems.at[0]
        ),
        pltpu.make_async_copy(
            power.at[pl.ds(me * BLOCKS, BLOCKS)], mine_power, local_sems.at[1]
        ),
        pltpu.make_async_copy(
            model.at[0, pl.ds(me * BLOCKS, BLOCKS)], got_model.at[me], local_sems.at[2]
        ),
        pltpu.make_async_copy(
            noise.at[0, pl.ds(me * BLOCKS, BLOCKS)], got_noise.at[me], local_sems.at[3]
        ),
        pltpu.make_async_copy(
            prior.at[0, pl.ds(me * BLOCKS, BLOCKS)], got_prior.at[me], local_sems.at[4]
        ),
    ]
    for copy in own:
        copy.start()

    barrier = pltpu.get_barrier_semaphore()
    for peer in peers:
        pl.semaphore_signal(barrier, inc=1, device_id=(peer, strip), device_id_type=MESH)
    for beside in (east, west):
        pl.semaphore_signal(barrier, inc=1, device_id=(me, beside), device_id_type=MESH)
    pl.semaphore_wait(barrier, len(peers) + 2)

    def push(src, dst, sem, peer, beside):
        pltpu.make_async_remote_copy(
            src_ref=src,
            dst_ref=dst,
            send_sem=send_sems.at[sem],
            recv_sem=recv_sems.at[sem],
            device_id=(peer, beside),
            device_id_type=MESH,
        ).start()

    for peer in peers:
        push(model.at[0, pl.ds(peer * BLOCKS, BLOCKS)], got_model.at[me], 0, peer, strip)
        push(noise.at[0, pl.ds(peer * BLOCKS, BLOCKS)], got_noise.at[me], 1, peer, strip)

    def push_prior(chunk):
        for peer in peers:
            push(
                prior.at[0, pl.ds(peer * BLOCKS + chunk * CHUNK, CHUNK)],
                got_prior.at[me, pl.ds(chunk * CHUNK, CHUNK)],
                2 + chunk,
                peer,
                strip,
            )

    push_prior(0)

    def wait_all(sems, sem, ref):
        pltpu.make_async_copy(ref, ref, sems.at[sem]).wait()

    for copy in own:
        copy.wait()
    others = pl.ds(0, MEMBERS - 1)
    wait_all(recv_sems, 0, got_model.at[others])
    wait_all(recv_sems, 1, got_noise.at[others])

    slots = lax.broadcasted_iota(jnp.int32, (1, CELLS), 1)
    for block in range(BLOCKS):
        forecast = got_model[:, block, :]
        drawn = got_noise[:, block, :]
        mismatch = mine_sensor[block : block + 1, :] + drawn - forecast
        anomaly = forecast - jnp.sum(forecast, axis=0, keepdims=True) / MEMBERS
        spread = jnp.sum(anomaly * anomaly, axis=0, keepdims=True) / (MEMBERS - 1)
        active = (slots < tally[me * BLOCKS + block]).astype(F32)
        weights = mismatch * (active / (spread + mine_power[block : block + 1, :]))
        product = lax.dot_general(
            weights,
            anomaly,
            (((1,), (1,)), ((), ())),
            precision=lax.Precision.HIGHEST,
            preferred_element_type=F32,
        )
        half = (block % 2) * MEMBERS
        products[1, block // 2, :, half : half + MEMBERS] = product

    def beside_copy(slot, beside):
        return pltpu.make_async_remote_copy(
            src_ref=products.at[1],
            dst_ref=products.at[slot],
            send_sem=strip_sems.at[0, slot // 2],
            recv_sem=strip_sems.at[1, slot // 2],
            device_id=(me, beside),
            device_id_type=MESH,
        )

    copies = [beside_copy(0, east), beside_copy(2, west)]
    for copy in copies:
        copy.start()
    for copy in copies:
        copy.wait()

    low = lax.broadcasted_iota(jnp.int32, (MEMBERS, CELLS), 1) < MEMBERS

    def part_of(tile, pair):
        folded = []
        for item in range(2):
            first = ((tile * BLOCKS) + pair * 2 + item) * 3 * BLOCKS
            total = jnp.zeros((MEMBERS, CELLS), F32)
            for beside in range(3):
                for both in range(BLOCKS // 2):
                    at = first + beside * BLOCKS + both * 2
                    total = total + products[beside, both] * jnp.where(low, select[at], select[at + 1])
            folded.append(total + pltpu.roll(total, MEMBERS, 1))
        return jnp.where(low, folded[0], folded[1])

    def fill(tile):
        def body(pair, carry):
            partial[tile, pair] = part_of(tile, pair)
            return carry

        lax.fori_loop(0, BLOCKS // 2, body, 0)

    def line_copy(tile, slot, peer):
        return pltpu.make_async_remote_copy(
            src_ref=partial.at[tile],
            dst_ref=got_partial.at[slot],
            send_sem=line_sems.at[0, slot],
            recv_sem=line_sems.at[1, slot],
            device_id=(peer, strip),
            device_id_type=MESH,
        )

    fill(0)
    down = line_copy(0, 0, south)
    down.start()
    fill(2)
    up = line_copy(2, 1, north)
    up.start()
    push_prior(1)
    fill(1)
    down.wait()
    up.wait()

    for pair in range(BLOCKS // 2):
        both = partial[1, pair] + got_partial[0, pair] + got_partial[1, pair]
        for item in range(2):
            one = both if item == 0 else pltpu.roll(both, MEMBERS, 1)
            one = one[:, 0:MEMBERS]
            one = one - jnp.sum(one, axis=1, keepdims=True) / MEMBERS
            high = one.astype(BF16)
            rest = one - high.astype(F32)
            middle = rest.astype(BF16)
            rest = rest - middle.astype(F32)
            mixing[pair * 2 + item, 0] = high
            mixing[pair * 2 + item, 1] = middle
            mixing[pair * 2 + item, 2] = rest.astype(BF16)

    for chunk in range(BLOCKS // CHUNK):
        wait_all(recv_sems, 2 + chunk, got_prior.at[others, pl.ds(0, CHUNK)])

        def body(step, carry):
            block = chunk * CHUNK + step
            wide_in[...] = got_prior[:, block].astype(F32).reshape(MEMBERS * LEVELS, CELLS)
            state = jnp.concatenate(
                [
                    wide_in[pl.ds(level, MEMBERS, stride=LEVELS), :].astype(BF16)
                    for level in range(LEVELS)
                ],
                axis=1,
            )
            total = jnp.zeros((MEMBERS, LEVELS * CELLS), F32)
            for term in (2, 1, 0):
                total = total + jnp.dot(mixing[block, term], state, preferred_element_type=F32)
            for level in range(LEVELS):
                wide_out[pl.ds(level, MEMBERS, stride=LEVELS), :] = total[
                    :, level * CELLS : (level + 1) * CELLS
                ]
            increment[:, block] = wide_out[...].reshape(MEMBERS, LEVELS, CELLS).astype(BF16)
            return carry

        lax.fori_loop(0, CHUNK, body, 0)
        part = pl.ds(chunk * CHUNK, CHUNK)
        landing = pl.ds(me * BLOCKS + chunk * CHUNK, CHUNK)
        for peer in peers:
            push(increment.at[peer, part], out.at[0, landing], 4 + chunk, peer, strip)
        pltpu.make_async_copy(
            increment.at[me, part], out.at[0, landing], local_sems.at[5 + chunk]
        ).start()

    for chunk in range(BLOCKS // CHUNK):
        part = pl.ds(chunk * CHUNK, CHUNK)
        landing = pl.ds(me * BLOCKS + chunk * CHUNK, CHUNK)
        pltpu.make_async_copy(
            increment.at[me, part], out.at[0, landing], local_sems.at[5 + chunk]
        ).wait()
    wait_all(send_sems, 0, got_model.at[others])
    wait_all(send_sems, 1, got_noise.at[others])
    for chunk in range(BLOCKS // CHUNK):
        for sem, sems in ((2 + chunk, (send_sems,)), (4 + chunk, (send_sems, recv_sems))):
            for each in sems:
                wait_all(each, sem, increment.at[others, pl.ds(0, CHUNK)])


def selection(neighbour_listing, sensor_patch_start):
    me = lax.axis_index("member")
    strip = lax.axis_index("space")
    around = jnp.arange(-1, 2, dtype=jnp.int32)
    tiles = neighbour_listing.reshape(MEMBERS, BLOCKS * BLOCKS)
    listed = jnp.concatenate(
        [
            lax.dynamic_slice_in_dim(tiles, lax.rem(me + shift + MEMBERS, MEMBERS), 1, 0)
            for shift in (-1, 0, 1)
        ]
    ).reshape(3, BLOCKS, 1, 1, BLOCKS)
    starts = lax.dynamic_slice_in_dim(
        sensor_patch_start.reshape(STRIPS, MEMBERS, BLOCKS), me, 1, 1
    )[:, 0]
    starts = jnp.concatenate(
        [
            lax.dynamic_slice_in_dim(starts, lax.rem(strip + shift + STRIPS, STRIPS), 1, 0)
            for shift in (-1, 0, 1)
        ]
    )[None, None]
    inner = jnp.arange(BLOCKS, dtype=jnp.int32)
    names = ((strip + around)[:, None] * MEMBERS + me) * BLOCKS + inner[None]
    hits = jnp.sum((listed == names[None, None, :, :, None]).astype(F32), axis=-1)
    delta_x = (strip * BLOCKS + inner)[None, :, None, None] - starts
    delta_x = delta_x.astype(F32)
    delta_y = around[:, None, None, None].astype(F32)
    distance = delta_x * delta_x + delta_y * delta_y
    taper = 1.0 / (1.0 + distance / float(BLOCKS * BLOCKS))
    return (taper * hits / (MEMBERS - 1)).reshape(-1)


def local(prior, model, noise, sensor, power, tally, start, listing):
    vmem, smem, anywhere = pltpu.VMEM, pltpu.SMEM, pl.ANY
    tile = (MEMBERS, BLOCKS, CELLS)
    state = (MEMBERS, BLOCKS, LEVELS, CELLS)
    packed = (BLOCKS // 2, MEMBERS, CELLS)
    dma = pltpu.SemaphoreType.DMA
    return pl.pallas_call(
        kernel,
        name="analysis",
        out_shape=jax.ShapeDtypeStruct(prior.shape, BF16),
        in_specs=[pl.BlockSpec(memory_space=anywhere)] * 5 + [pl.BlockSpec(memory_space=smem)] * 2,
        out_specs=pl.BlockSpec(memory_space=vmem),
        scratch_shapes=[
            vmem(tile, F32),
            vmem(tile, F32),
            vmem(state, BF16),
            vmem((BLOCKS, CELLS), F32),
            vmem((BLOCKS, CELLS), F32),
            vmem((3, *packed), F32),
            vmem((3, *packed), F32),
            vmem((2, *packed), F32),
            vmem((BLOCKS, 3, MEMBERS, MEMBERS), BF16),
            vmem((MEMBERS * LEVELS, CELLS), F32),
            vmem((MEMBERS * LEVELS, CELLS), F32),
            vmem(state, BF16),
            dma((6,)),
            dma((6,)),
            dma((7,)),
            dma((2, 2)),
            dma((2, 2)),
        ],
        compiler_params=pltpu.CompilerParams(collective_id=0, has_side_effects=True),
    )(prior, model, noise, sensor, power, tally, selection(listing, start))


def solution(mesh):
    placed = (
        P("member", "space", None, None),
        P("member", "space", None),
        P("member", "space", None),
        P("space", None),
        P("space", None),
        P("space"),
        P(),
        P("space", None),
    )
    return jax.shard_map(
        local,
        mesh=mesh,
        in_specs=placed,
        out_specs=P("member", "space", None, None),
        check_vma=False,
    )
```

```python
import jax
import jax.numpy as jnp
from jax import lax
from jax.experimental import pallas as pl
from jax.experimental.pallas import tpu as pltpu
from jax.sharding import PartitionSpec as P

MESH = pl.DeviceIdType.MESH
SIDE = 8
MEMBERS = 64
STRIPS = 8
BLOCKS = 8
LEVELS = 8
CELLS = 128
CHUNK = 2
CHUNKS = BLOCKS // CHUNK
EARLY = 2
BEFORE = 3
ACROSS = (4, 3, 5, 2, 6, 1, 7, 0)
F32 = jnp.float32
BF16 = jnp.bfloat16


def far_first():
    def span(a):
        return min(a, SIDE - a)

    def rank(offset):
        a, b = span(offset[0]), span(offset[1])
        return (-(a + b), -max(a, b), min(offset))

    offsets = [(a, b) for a in range(SIDE) for b in range(SIDE) if (a, b) != (0, 0)]
    return sorted(offsets, key=rank)


OFFSETS = far_first()


def kernel(
    prior,
    model,
    noise,
    sensor,
    power,
    tally_hbm,
    start_hbm,
    listing_hbm,
    out,
    got_model,
    got_noise,
    got_prior,
    mine_sensor,
    mine_power,
    listing,
    tally,
    start,
    pattern,
    products,
    partial,
    got_partial,
    mixing,
    wide_in,
    wide_out,
    increment,
    send_sems,
    recv_sems,
    local_sems,
    strip_sems,
    line_sems,
    row_sems,
):
    me = lax.axis_index("member")
    strip = lax.axis_index("space")
    row, column = me // SIDE, lax.rem(me, SIDE)

    def member(offset):
        return lax.rem(row + offset[0], SIDE) * SIDE + lax.rem(column + offset[1], SIDE)

    peers = [member(offset) for offset in OFFSETS]
    east, west = lax.rem(strip + 1, STRIPS), lax.rem(strip + STRIPS - 1, STRIPS)
    north, south = lax.rem(me + 1, MEMBERS), lax.rem(me + MEMBERS - 1, MEMBERS)

    barrier = pltpu.get_barrier_semaphore()
    for peer in peers:
        pl.semaphore_signal(barrier, inc=1, device_id=(peer, strip), device_id_type=MESH)
    for beside in (east, west):
        pl.semaphore_signal(barrier, inc=1, device_id=(me, beside), device_id_type=MESH)

    mine = pl.ds(me * BLOCKS, BLOCKS)
    own = [
        pltpu.make_async_copy(src, dst, local_sems.at[at])
        for at, (src, dst) in enumerate(
            (
                (start_hbm, start),
                (tally_hbm, tally),
                (listing_hbm, listing),
                (sensor.at[mine], mine_sensor),
                (power.at[mine], mine_power),
                (model.at[0, mine], got_model.at[me]),
                (noise.at[0, mine], got_noise.at[me]),
                (prior.at[0, mine], got_prior.at[me]),
            )
        )
    ]
    for copy in own:
        copy.start()

    def push(src, dst, sem, peer, beside):
        pltpu.make_async_remote_copy(
            src_ref=src,
            dst_ref=dst,
            send_sem=send_sems.at[sem],
            recv_sem=recv_sems.at[sem],
            device_id=(peer, beside),
            device_id_type=MESH,
        ).start()

    def push_readings(peer):
        theirs = pl.ds(peer * BLOCKS, BLOCKS)
        push(model.at[0, theirs], got_model.at[me], 0, peer, strip)
        push(noise.at[0, theirs], got_noise.at[me], 1, peer, strip)

    def push_prior(chunk, peer):
        push(
            prior.at[0, pl.ds(peer * BLOCKS + chunk * CHUNK, CHUNK)],
            got_prior.at[me, pl.ds(chunk * CHUNK, CHUNK)],
            2 + chunk,
            peer,
            strip,
        )

    def early(peer):
        for chunk in range(EARLY):
            push_prior(chunk, peer)

    def to_row(target, *actions):
        for shift in ACROSS:
            peer = target * SIDE + lax.rem(column + shift, SIDE)

            def act(peer=peer):
                for action in actions:
                    action(peer)

            if shift == 0:
                pl.when(target != row)(act)
            else:
                act()

    pl.semaphore_wait(barrier, len(peers) + 2)

    def there(action):
        def body(at, carry):
            to_row(row - at, action)
            return carry

        lax.fori_loop(0, row + 1, body, 0)

    for peer in peers:
        push_readings(peer)
    for chunk in range(EARLY):
        for peer in peers:
            push_prior(chunk, peer)

    def wait_all(sems, sem, ref):
        pltpu.make_async_copy(ref, ref, sems.at[sem]).wait()

    for copy in own:
        copy.wait()

    around = 3 * BLOCKS
    tall, long = (around, CELLS), (around, MEMBERS * BLOCKS)
    which = lax.broadcasted_iota(jnp.int32, tall, 0)
    begins = jnp.zeros(tall, jnp.int32)
    for at in range(around):
        tile = lax.rem(strip + at // BLOCKS + STRIPS - 1, STRIPS) * MEMBERS + me
        begins = jnp.where(which == at, start[tile * BLOCKS + at % BLOCKS], begins)
    begins = jnp.concatenate([begins] * (MEMBERS * BLOCKS // CELLS), axis=1)
    which = lax.broadcasted_iota(jnp.int32, long, 0)
    state = lax.broadcasted_iota(jnp.int32, long, 1)
    names = ((strip + (which >> 3) - 1) * MEMBERS + me) * BLOCKS + (which & 7)
    hits = jnp.zeros(long, F32)
    for at in range(BLOCKS):
        hits = hits + jnp.where(listing[at : at + 1, :] == names, 1.0, 0.0)
    delta_x = (strip * BLOCKS + (state & 7) - begins).astype(F32)
    delta_y = ((state >> 3) - me).astype(F32)
    distance = delta_x * delta_x + delta_y * delta_y
    taper = hits * (1.0 / (1.0 + distance * (1.0 / (BLOCKS * BLOCKS)))) * (1.0 / (MEMBERS - 1))
    tile = me + (which >> 3) - 1
    tile = jnp.where(tile < 0, tile + MEMBERS, jnp.where(tile >= MEMBERS, tile - MEMBERS, tile))
    chosen = (state == tile * BLOCKS + (which & 7)).astype(F32)
    factors = lax.dot_general(
        chosen,
        taper,
        (((1,), (1,)), ((), ())),
        precision=lax.Precision.HIGHEST,
        preferred_element_type=F32,
    )
    spread_to = (around, around * MEMBERS)
    lanes = lax.broadcasted_iota(jnp.int32, spread_to, 1) >> 6
    place = (lax.broadcasted_iota(jnp.int32, spread_to, 0) == lanes).astype(F32)
    spread_out = jnp.dot(
        factors, place, precision=lax.Precision.HIGHEST, preferred_element_type=F32
    )
    for both in range(around // 2):
        pattern[:, both, :] = spread_out[:, both * CELLS : (both + 1) * CELLS]

    others = pl.ds(0, MEMBERS - 1)
    wait_all(recv_sems, 0, got_model.at[others])
    wait_all(recv_sems, 1, got_noise.at[others])
    for peer in peers:
        for chunk in range(EARLY, BEFORE):
            push_prior(chunk, peer)

    slots = lax.broadcasted_iota(jnp.int32, (1, CELLS), 1)
    for block in range(BLOCKS):
        forecast = got_model[:, block, :]
        drawn = got_noise[:, block, :]
        mismatch = mine_sensor[block : block + 1, :] + drawn - forecast
        anomaly = forecast - jnp.sum(forecast, axis=0, keepdims=True) / MEMBERS
        spread = jnp.sum(anomaly * anomaly, axis=0, keepdims=True) / (MEMBERS - 1)
        active = (slots < tally[me * BLOCKS + block]).astype(F32)
        weights = mismatch * (active / (spread + mine_power[block : block + 1, :]))
        product = lax.dot_general(
            weights,
            anomaly,
            (((1,), (1,)), ((), ())),
            precision=lax.Precision.HIGHEST,
            preferred_element_type=F32,
        )
        half = (block % 2) * MEMBERS
        products[1, block // 2, :, half : half + MEMBERS] = product

    def beside_copy(slot, beside):
        return pltpu.make_async_remote_copy(
            src_ref=products.at[1],
            dst_ref=products.at[slot],
            send_sem=strip_sems.at[0, slot // 2],
            recv_sem=strip_sems.at[1, slot // 2],
            device_id=(me, beside),
            device_id_type=MESH,
        )

    copies = [beside_copy(0, east), beside_copy(2, west)]
    for copy in copies:
        copy.start()
    for copy in copies:
        copy.wait()

    low = lax.broadcasted_iota(jnp.int32, (MEMBERS, CELLS), 1) < MEMBERS

    def part_of(tile, pair):
        folded = []
        for item in range(2):
            at = tile * BLOCKS + pair * 2 + item
            total = jnp.zeros((MEMBERS, CELLS), F32)
            for both in range(around // 2):
                factor = pattern[at, both : both + 1, :]
                total = total + products[both // (BLOCKS // 2), both % (BLOCKS // 2)] * factor
            folded.append(total + pltpu.roll(total, MEMBERS, 1))
        return jnp.where(low, folded[0], folded[1])

    def fill(tile):
        def body(pair, carry):
            partial[tile, pair] = part_of(tile, pair)
            return carry

        lax.fori_loop(0, BLOCKS // 2, body, 0)

    def line_copy(tile, slot, peer):
        return pltpu.make_async_remote_copy(
            src_ref=partial.at[tile],
            dst_ref=got_partial.at[slot],
            send_sem=line_sems.at[0, slot],
            recv_sem=line_sems.at[1, slot],
            device_id=(peer, strip),
            device_id_type=MESH,
        )

    fill(0)
    down = line_copy(0, 0, south)
    down.start()
    fill(2)
    up = line_copy(2, 1, north)
    up.start()
    for peer in peers:
        for chunk in range(BEFORE, CHUNKS):
            push_prior(chunk, peer)
    fill(1)
    down.wait()
    up.wait()

    for pair in range(BLOCKS // 2):
        both = partial[1, pair] + got_partial[0, pair] + got_partial[1, pair]
        for item in range(2):
            one = both if item == 0 else pltpu.roll(both, MEMBERS, 1)
            one = one[:, 0:MEMBERS]
            one = one - jnp.sum(one, axis=1, keepdims=True) / MEMBERS
            high = one.astype(BF16)
            rest = one - high.astype(F32)
            middle = rest.astype(BF16)
            rest = rest - middle.astype(F32)
            mixing[pair * 2 + item, 0] = high
            mixing[pair * 2 + item, 1] = middle
            mixing[pair * 2 + item, 2] = rest.astype(BF16)

    def landed(chunk):
        return pltpu.make_async_copy(
            increment.at[me, pl.ds(chunk * CHUNK, CHUNK)],
            out.at[0, pl.ds(me * BLOCKS + chunk * CHUNK, CHUNK)],
            local_sems.at[8 + chunk],
        )

    for chunk in range(CHUNKS):
        wait_all(recv_sems, 2 + chunk, got_prior.at[others, pl.ds(0, CHUNK)])

        def body(step, carry):
            block = chunk * CHUNK + step
            wide_in[...] = got_prior[:, block].astype(F32).reshape(MEMBERS * LEVELS, CELLS)
            state = jnp.concatenate(
                [
                    wide_in[pl.ds(level, MEMBERS, stride=LEVELS), :].astype(BF16)
                    for level in range(LEVELS)
                ],
                axis=1,
            )
            total = jnp.zeros((MEMBERS, LEVELS * CELLS), F32)
            for term in (2, 1, 0):
                total = total + jnp.dot(mixing[block, term], state, preferred_element_type=F32)
            for level in range(LEVELS):
                wide_out[pl.ds(level, MEMBERS, stride=LEVELS), :] = total[
                    :, level * CELLS : (level + 1) * CELLS
                ]
            increment[:, block] = wide_out[...].reshape(MEMBERS, LEVELS, CELLS).astype(BF16)
            return carry

        lax.fori_loop(0, CHUNK, body, 0)
        part = pl.ds(chunk * CHUNK, CHUNK)
        landing = pl.ds(me * BLOCKS + chunk * CHUNK, CHUNK)
        for peer in peers:
            push(increment.at[peer, part], out.at[0, landing], 2 + CHUNKS + chunk, peer, strip)
        landed(chunk).start()

    for chunk in range(CHUNKS):
        landed(chunk).wait()
    wait_all(send_sems, 0, got_model.at[others])
    wait_all(send_sems, 1, got_noise.at[others])
    one = increment.at[others, pl.ds(0, CHUNK)]
    for chunk in range(CHUNKS):
        wait_all(send_sems, 2 + chunk, one)
        wait_all(send_sems, 2 + CHUNKS + chunk, one)
        wait_all(recv_sems, 2 + CHUNKS + chunk, one)


def local(prior, model, noise, sensor, power, tally, start, listing):
    vmem, smem, anywhere = pltpu.VMEM, pltpu.SMEM, pl.ANY
    tile = (MEMBERS, BLOCKS, CELLS)
    state = (MEMBERS, BLOCKS, LEVELS, CELLS)
    packed = (BLOCKS // 2, MEMBERS, CELLS)
    dma = pltpu.SemaphoreType.DMA
    return pl.pallas_call(
        kernel,
        name="analysis",
        out_shape=vmem(prior.shape, BF16),
        in_specs=[pl.BlockSpec(memory_space=anywhere)] * 8,
        out_specs=pl.BlockSpec(memory_space=vmem),
        scratch_shapes=[
            vmem(tile, F32),
            vmem(tile, F32),
            vmem(state, BF16),
            vmem((BLOCKS, CELLS), F32),
            vmem((BLOCKS, CELLS), F32),
            vmem((BLOCKS, MEMBERS * BLOCKS), jnp.int32),
            smem((MEMBERS * BLOCKS,), jnp.int32),
            smem((STRIPS * MEMBERS * BLOCKS,), jnp.int32),
            vmem((3 * BLOCKS, 3 * BLOCKS // 2, CELLS), F32),
            vmem((3, *packed), F32),
            vmem((3, *packed), F32),
            vmem((2, *packed), F32),
            vmem((BLOCKS, 3, MEMBERS, MEMBERS), BF16),
            vmem((MEMBERS * LEVELS, CELLS), F32),
            vmem((MEMBERS * LEVELS, CELLS), F32),
            vmem(state, BF16),
            dma((2 + 2 * CHUNKS,)),
            dma((2 + 2 * CHUNKS,)),
            dma((8 + CHUNKS,)),
            dma((2, 2)),
            dma((2, 2)),
            pltpu.SemaphoreType.REGULAR((SIDE,)),
        ],
        compiler_params=pltpu.CompilerParams(collective_id=0, has_side_effects=True),
    )(prior, model, noise, sensor, power, tally, start, listing.T)


def solution(mesh):
    placed = (
        P("member", "space", None, None),
        P("member", "space", None),
        P("member", "space", None),
        P("space", None),
        P("space", None),
        P("space"),
        P(),
        P("space", None),
    )
    return jax.shard_map(
        local,
        mesh=mesh,
        in_specs=placed,
        out_specs=P("member", "space", None, None),
        check_vma=False,
    )
```

```python
import jax
import jax.numpy as jnp
from jax import lax
from jax.experimental import pallas as pl
from jax.experimental.pallas import tpu as pltpu
from jax.sharding import PartitionSpec as P

MESH = pl.DeviceIdType.MESH
SIDE = 8
MEMBERS = 64
STRIPS = 8
BLOCKS = 8
LEVELS = 8
CELLS = 128
CHUNK = 2
CHUNKS = BLOCKS // CHUNK
EARLY = 3
BEFORE = 3
MODEL_STEPS = float(1 << 20)
NOISE_STEPS = float(1 << 19)
F32 = jnp.float32
BF16 = jnp.bfloat16


def far_first():
    def span(a):
        return min(a, SIDE - a)

    def rank(offset):
        a, b = span(offset[0]), span(offset[1])
        return (-(a + b), -max(a, b), min(offset))

    offsets = [(a, b) for a in range(SIDE) for b in range(SIDE) if (a, b) != (0, 0)]
    return sorted(offsets, key=rank)


OFFSETS = far_first()


def kernel(
    prior,
    model,
    noise,
    sensor,
    power,
    tally_hbm,
    start_hbm,
    listing_hbm,
    out,
    raw_model,
    raw_noise,
    coded,
    got_coded,
    got_model,
    got_noise,
    got_prior,
    mine_sensor,
    mine_power,
    listing,
    tally,
    start,
    pattern,
    products,
    partial,
    got_partial,
    mixing,
    wide_in,
    wide_out,
    increment,
    send_sems,
    recv_sems,
    local_sems,
    strip_sems,
    line_sems,
):
    me = lax.axis_index("member")
    strip = lax.axis_index("space")
    row, column = me // SIDE, lax.rem(me, SIDE)

    def member(offset):
        return lax.rem(row + offset[0], SIDE) * SIDE + lax.rem(column + offset[1], SIDE)

    peers = [member(offset) for offset in OFFSETS]
    east, west = lax.rem(strip + 1, STRIPS), lax.rem(strip + STRIPS - 1, STRIPS)
    north, south = lax.rem(me + 1, MEMBERS), lax.rem(me + MEMBERS - 1, MEMBERS)

    barrier = pltpu.get_barrier_semaphore()
    for peer in peers:
        pl.semaphore_signal(barrier, inc=1, device_id=(peer, strip), device_id_type=MESH)
    for beside in (east, west):
        pl.semaphore_signal(barrier, inc=1, device_id=(me, beside), device_id_type=MESH)

    mine = pl.ds(me * BLOCKS, BLOCKS)
    own = [
        pltpu.make_async_copy(src, dst, local_sems.at[at])
        for at, (src, dst) in enumerate(
            (
                (start_hbm, start),
                (tally_hbm, tally),
                (listing_hbm, listing),
                (sensor.at[mine], mine_sensor),
                (power.at[mine], mine_power),
                (prior.at[0, mine], got_prior.at[me]),
                (model.at[0], raw_model),
                (noise.at[0], raw_noise),
            )
        )
    ]
    for copy in own:
        copy.start()

    def push(src, dst, sem, peer, beside):
        pltpu.make_async_remote_copy(
            src_ref=src,
            dst_ref=dst,
            send_sem=send_sems.at[sem],
            recv_sem=recv_sems.at[sem],
            device_id=(peer, beside),
            device_id_type=MESH,
        ).start()

    def push_readings(peer):
        push(coded.at[peer], got_coded.at[me], 0, peer, strip)

    def push_prior(chunk, peer):
        push(
            prior.at[0, pl.ds(peer * BLOCKS + chunk * CHUNK, CHUNK)],
            got_prior.at[me, pl.ds(chunk * CHUNK, CHUNK)],
            2 + chunk,
            peer,
            strip,
        )

    for copy in own[-2:]:
        copy.wait()

    def encode(at, carry):
        rows = pl.ds(at * CELLS, CELLS)
        tiles = pl.ds(at * (CELLS // BLOCKS), CELLS // BLOCKS)
        shape = (CELLS // BLOCKS, BLOCKS, CELLS)
        first = jnp.floor(raw_model[rows, :] * MODEL_STEPS + 0.5).astype(jnp.int32)
        second = jnp.floor(raw_noise[rows, :] * NOISE_STEPS + 0.5).astype(jnp.int32)
        low = ((first & 255) << 8) + (second & 255) - 32768
        for word, value in enumerate((first >> 8, second >> 8, low)):
            coded[tiles, word] = value.reshape(shape).astype(jnp.int16)
        return carry

    lax.fori_loop(0, MEMBERS * BLOCKS // CELLS, encode, 0)
    kept = pltpu.make_async_copy(coded.at[me], got_coded.at[me], local_sems.at[8 + CHUNKS])
    kept.start()

    pl.semaphore_wait(barrier, len(peers) + 2)
    for peer in peers:
        push_readings(peer)
    for chunk in range(EARLY):
        for peer in peers:
            push_prior(chunk, peer)

    def wait_all(sems, sem, ref):
        pltpu.make_async_copy(ref, ref, sems.at[sem]).wait()

    for copy in own[:-2]:
        copy.wait()
    kept.wait()

    around = 3 * BLOCKS
    tall, long = (around, CELLS), (around, MEMBERS * BLOCKS)
    which = lax.broadcasted_iota(jnp.int32, tall, 0)
    begins = jnp.zeros(tall, jnp.int32)
    for at in range(around):
        tile = lax.rem(strip + at // BLOCKS + STRIPS - 1, STRIPS) * MEMBERS + me
        begins = jnp.where(which == at, start[tile * BLOCKS + at % BLOCKS], begins)
    begins = jnp.concatenate([begins] * (MEMBERS * BLOCKS // CELLS), axis=1)
    which = lax.broadcasted_iota(jnp.int32, long, 0)
    state = lax.broadcasted_iota(jnp.int32, long, 1)
    names = ((strip + (which >> 3) - 1) * MEMBERS + me) * BLOCKS + (which & 7)
    hits = jnp.zeros(long, F32)
    for at in range(BLOCKS):
        hits = hits + jnp.where(listing[at : at + 1, :] == names, 1.0, 0.0)
    delta_x = (strip * BLOCKS + (state & 7) - begins).astype(F32)
    delta_y = ((state >> 3) - me).astype(F32)
    distance = delta_x * delta_x + delta_y * delta_y
    taper = hits * (1.0 / (1.0 + distance * (1.0 / (BLOCKS * BLOCKS)))) * (1.0 / (MEMBERS - 1))
    tile = me + (which >> 3) - 1
    tile = jnp.where(tile < 0, tile + MEMBERS, jnp.where(tile >= MEMBERS, tile - MEMBERS, tile))
    chosen = (state == tile * BLOCKS + (which & 7)).astype(F32)
    factors = lax.dot_general(
        chosen,
        taper,
        (((1,), (1,)), ((), ())),
        precision=lax.Precision.HIGHEST,
        preferred_element_type=F32,
    )
    spread_to = (around, around * MEMBERS)
    lanes = lax.broadcasted_iota(jnp.int32, spread_to, 1) >> 6
    place = (lax.broadcasted_iota(jnp.int32, spread_to, 0) == lanes).astype(F32)
    spread_out = jnp.dot(
        factors, place, precision=lax.Precision.HIGHEST, preferred_element_type=F32
    )
    for both in range(around // 2):
        pattern[:, both, :] = spread_out[:, both * CELLS : (both + 1) * CELLS]

    others = pl.ds(0, MEMBERS - 1)
    wait_all(recv_sems, 0, got_coded.at[others])
    for peer in peers:
        for chunk in range(EARLY, BEFORE):
            push_prior(chunk, peer)

    def decode(at, carry):
        group = pl.ds(at * BLOCKS, BLOCKS)
        first, second, low = (got_coded[group, word].astype(jnp.int32) for word in range(3))
        low = low + 32768
        got_model[group] = ((first << 8) + (low >> 8)).astype(F32) * (1.0 / MODEL_STEPS)
        got_noise[group] = ((second << 8) + (low & 255)).astype(F32) * (1.0 / NOISE_STEPS)
        return carry

    lax.fori_loop(0, MEMBERS // BLOCKS, decode, 0)

    slots = lax.broadcasted_iota(jnp.int32, (1, CELLS), 1)
    for block in range(BLOCKS):
        forecast = got_model[:, block, :]
        drawn = got_noise[:, block, :]
        mismatch = mine_sensor[block : block + 1, :] + drawn - forecast
        anomaly = forecast - jnp.sum(forecast, axis=0, keepdims=True) / MEMBERS
        spread = jnp.sum(anomaly * anomaly, axis=0, keepdims=True) / (MEMBERS - 1)
        active = (slots < tally[me * BLOCKS + block]).astype(F32)
        weights = mismatch * (active / (spread + mine_power[block : block + 1, :]))
        product = lax.dot_general(
            weights,
            anomaly,
            (((1,), (1,)), ((), ())),
            precision=lax.Precision.HIGHEST,
            preferred_element_type=F32,
        )
        half = (block % 2) * MEMBERS
        products[1, block // 2, :, half : half + MEMBERS] = product

    def beside_copy(slot, beside):
        return pltpu.make_async_remote_copy(
            src_ref=products.at[1],
            dst_ref=products.at[slot],
            send_sem=strip_sems.at[0, slot // 2],
            recv_sem=strip_sems.at[1, slot // 2],
            device_id=(me, beside),
            device_id_type=MESH,
        )

    copies = [beside_copy(0, east), beside_copy(2, west)]
    for copy in copies:
        copy.start()
    for copy in copies:
        copy.wait()

    low = lax.broadcasted_iota(jnp.int32, (MEMBERS, CELLS), 1) < MEMBERS

    def part_of(tile, pair):
        folded = []
        for item in range(2):
            at = tile * BLOCKS + pair * 2 + item
            total = jnp.zeros((MEMBERS, CELLS), F32)
            for both in range(around // 2):
                factor = pattern[at, both : both + 1, :]
                total = total + products[both // (BLOCKS // 2), both % (BLOCKS // 2)] * factor
            folded.append(total + pltpu.roll(total, MEMBERS, 1))
        return jnp.where(low, folded[0], folded[1])

    def fill(tile):
        def body(pair, carry):
            partial[tile, pair] = part_of(tile, pair)
            return carry

        lax.fori_loop(0, BLOCKS // 2, body, 0)

    def line_copy(tile, slot, peer):
        return pltpu.make_async_remote_copy(
            src_ref=partial.at[tile],
            dst_ref=got_partial.at[slot],
            send_sem=line_sems.at[0, slot],
            recv_sem=line_sems.at[1, slot],
            device_id=(peer, strip),
            device_id_type=MESH,
        )

    fill(0)
    down = line_copy(0, 0, south)
    down.start()
    fill(2)
    up = line_copy(2, 1, north)
    up.start()
    for peer in peers:
        for chunk in range(BEFORE, CHUNKS):
            push_prior(chunk, peer)
    fill(1)
    down.wait()
    up.wait()

    for pair in range(BLOCKS // 2):
        both = partial[1, pair] + got_partial[0, pair] + got_partial[1, pair]
        for item in range(2):
            one = both if item == 0 else pltpu.roll(both, MEMBERS, 1)
            one = one[:, 0:MEMBERS]
            one = one - jnp.sum(one, axis=1, keepdims=True) / MEMBERS
            high = one.astype(BF16)
            rest = one - high.astype(F32)
            middle = rest.astype(BF16)
            rest = rest - middle.astype(F32)
            mixing[pair * 2 + item, 0] = high
            mixing[pair * 2 + item, 1] = middle
            mixing[pair * 2 + item, 2] = rest.astype(BF16)

    def landed(chunk):
        return pltpu.make_async_copy(
            increment.at[me, pl.ds(chunk * CHUNK, CHUNK)],
            out.at[0, pl.ds(me * BLOCKS + chunk * CHUNK, CHUNK)],
            local_sems.at[8 + chunk],
        )

    for chunk in range(CHUNKS):
        wait_all(recv_sems, 2 + chunk, got_prior.at[others, pl.ds(0, CHUNK)])

        def body(step, carry):
            block = chunk * CHUNK + step
            wide_in[...] = got_prior[:, block].astype(F32).reshape(MEMBERS * LEVELS, CELLS)
            state = jnp.concatenate(
                [
                    wide_in[pl.ds(level, MEMBERS, stride=LEVELS), :].astype(BF16)
                    for level in range(LEVELS)
                ],
                axis=1,
            )
            total = jnp.zeros((MEMBERS, LEVELS * CELLS), F32)
            for term in (2, 1, 0):
                total = total + jnp.dot(mixing[block, term], state, preferred_element_type=F32)
            for level in range(LEVELS):
                wide_out[pl.ds(level, MEMBERS, stride=LEVELS), :] = total[
                    :, level * CELLS : (level + 1) * CELLS
                ]
            increment[:, block] = wide_out[...].reshape(MEMBERS, LEVELS, CELLS).astype(BF16)
            return carry

        lax.fori_loop(0, CHUNK, body, 0)
        part = pl.ds(chunk * CHUNK, CHUNK)
        landing = pl.ds(me * BLOCKS + chunk * CHUNK, CHUNK)
        for peer in peers:
            push(increment.at[peer, part], out.at[0, landing], 2 + CHUNKS + chunk, peer, strip)
        landed(chunk).start()

    for chunk in range(CHUNKS):
        landed(chunk).wait()
    wait_all(send_sems, 0, got_coded.at[others])
    one = increment.at[others, pl.ds(0, CHUNK)]
    for chunk in range(CHUNKS):
        wait_all(send_sems, 2 + chunk, one)
        wait_all(send_sems, 2 + CHUNKS + chunk, one)
        wait_all(recv_sems, 2 + CHUNKS + chunk, one)


def local(prior, model, noise, sensor, power, tally, start, listing):
    vmem, smem, anywhere = pltpu.VMEM, pltpu.SMEM, pl.ANY
    tile = (MEMBERS, BLOCKS, CELLS)
    state = (MEMBERS, BLOCKS, LEVELS, CELLS)
    packed = (BLOCKS // 2, MEMBERS, CELLS)
    dma = pltpu.SemaphoreType.DMA
    return pl.pallas_call(
        kernel,
        name="analysis",
        out_shape=vmem(prior.shape, BF16),
        in_specs=[pl.BlockSpec(memory_space=anywhere)] * 8,
        out_specs=pl.BlockSpec(memory_space=vmem),
        scratch_shapes=[
            vmem((MEMBERS * BLOCKS, CELLS), F32),
            vmem((MEMBERS * BLOCKS, CELLS), F32),
            vmem((MEMBERS, 3, BLOCKS, CELLS), jnp.int16),
            vmem((MEMBERS, 3, BLOCKS, CELLS), jnp.int16),
            vmem(tile, F32),
            vmem(tile, F32),
            vmem(state, BF16),
            vmem((BLOCKS, CELLS), F32),
            vmem((BLOCKS, CELLS), F32),
            vmem((BLOCKS, MEMBERS * BLOCKS), jnp.int32),
            smem((MEMBERS * BLOCKS,), jnp.int32),
            smem((STRIPS * MEMBERS * BLOCKS,), jnp.int32),
            vmem((3 * BLOCKS, 3 * BLOCKS // 2, CELLS), F32),
            vmem((3, *packed), F32),
            vmem((3, *packed), F32),
            vmem((2, *packed), F32),
            vmem((BLOCKS, 3, MEMBERS, MEMBERS), BF16),
            vmem((MEMBERS * LEVELS, CELLS), F32),
            vmem((MEMBERS * LEVELS, CELLS), F32),
            vmem(state, BF16),
            dma((2 + 2 * CHUNKS,)),
            dma((2 + 2 * CHUNKS,)),
            dma((9 + CHUNKS,)),
            dma((2, 2)),
            dma((2, 2)),
        ],
        compiler_params=pltpu.CompilerParams(collective_id=0, has_side_effects=True),
    )(prior, model, noise, sensor, power, tally, start, listing.T)


def solution(mesh):
    placed = (
        P("member", "space", None, None),
        P("member", "space", None),
        P("member", "space", None),
        P("space", None),
        P("space", None),
        P("space"),
        P(),
        P("space", None),
    )
    return jax.shard_map(
        local,
        mesh=mesh,
        in_specs=placed,
        out_specs=P("member", "space", None, None),
        check_vma=False,
    )
```

```python
import jax
import jax.numpy as jnp
from jax import lax
from jax.experimental import pallas as pl
from jax.experimental.pallas import tpu as pltpu
from jax.sharding import PartitionSpec as P

MESH = pl.DeviceIdType.MESH
SIDE = 8
MEMBERS = 64
STRIPS = 8
BLOCKS = 8
LEVELS = 8
CELLS = 128
CHUNK = 2
CHUNKS = BLOCKS // CHUNK
EARLY = 3
BEFORE = 3
MODEL_STEPS = float(1 << 20)
NOISE_STEPS = float(1 << 19)
LINE_STEPS = float((1 << 19) - 1)
F32 = jnp.float32
BF16 = jnp.bfloat16


def far_first():
    def span(a):
        return min(a, SIDE - a)

    def rank(offset):
        a, b = span(offset[0]), span(offset[1])
        return (-(a + b), -max(a, b), min(offset))

    offsets = [(a, b) for a in range(SIDE) for b in range(SIDE) if (a, b) != (0, 0)]
    return sorted(offsets, key=rank)


OFFSETS = far_first()


def kernel(
    prior,
    model,
    noise,
    sensor,
    power,
    tally_hbm,
    start_hbm,
    listing_hbm,
    out,
    raw_model,
    raw_noise,
    coded,
    got_coded,
    got_model,
    got_noise,
    got_prior,
    mine_sensor,
    mine_power,
    listing,
    tally,
    start,
    pattern,
    products,
    partial,
    line_out,
    line_in,
    line_unit,
    got_unit,
    mixing,
    wide_in,
    wide_out,
    increment,
    send_sems,
    recv_sems,
    local_sems,
    strip_sems,
    line_sems,
):
    me = lax.axis_index("member")
    strip = lax.axis_index("space")
    row, column = me // SIDE, lax.rem(me, SIDE)

    def member(offset):
        return lax.rem(row + offset[0], SIDE) * SIDE + lax.rem(column + offset[1], SIDE)

    peers = [member(offset) for offset in OFFSETS]
    east, west = lax.rem(strip + 1, STRIPS), lax.rem(strip + STRIPS - 1, STRIPS)
    north, south = lax.rem(me + 1, MEMBERS), lax.rem(me + MEMBERS - 1, MEMBERS)

    barrier = pltpu.get_barrier_semaphore()
    for peer in peers:
        pl.semaphore_signal(barrier, inc=1, device_id=(peer, strip), device_id_type=MESH)
    for beside in (east, west):
        pl.semaphore_signal(barrier, inc=1, device_id=(me, beside), device_id_type=MESH)

    mine = pl.ds(me * BLOCKS, BLOCKS)
    own = [
        pltpu.make_async_copy(src, dst, local_sems.at[at])
        for at, (src, dst) in enumerate(
            (
                (start_hbm, start),
                (tally_hbm, tally),
                (listing_hbm, listing),
                (sensor.at[mine], mine_sensor),
                (power.at[mine], mine_power),
                (prior.at[0, mine], got_prior.at[me]),
                (model.at[0], raw_model),
                (noise.at[0], raw_noise),
            )
        )
    ]
    for copy in own:
        copy.start()

    def push(src, dst, sem, peer, beside):
        pltpu.make_async_remote_copy(
            src_ref=src,
            dst_ref=dst,
            send_sem=send_sems.at[sem],
            recv_sem=recv_sems.at[sem],
            device_id=(peer, beside),
            device_id_type=MESH,
        ).start()

    def push_readings(peer):
        push(coded.at[peer], got_coded.at[me], 0, peer, strip)

    def push_prior(chunk, peer):
        push(
            prior.at[0, pl.ds(peer * BLOCKS + chunk * CHUNK, CHUNK)],
            got_prior.at[me, pl.ds(chunk * CHUNK, CHUNK)],
            2 + chunk,
            peer,
            strip,
        )

    for copy in own[-2:]:
        copy.wait()

    def encode(at, carry):
        rows = pl.ds(at * CELLS, CELLS)
        tiles = pl.ds(at * (CELLS // BLOCKS), CELLS // BLOCKS)
        shape = (CELLS // BLOCKS, BLOCKS, CELLS)
        first = jnp.floor(raw_model[rows, :] * MODEL_STEPS + 0.5).astype(jnp.int32)
        second = jnp.floor(raw_noise[rows, :] * NOISE_STEPS + 0.5).astype(jnp.int32)
        low = ((first & 255) << 8) + (second & 255) - 32768
        for word, value in enumerate((first >> 8, second >> 8, low)):
            coded[tiles, word] = value.reshape(shape).astype(jnp.int16)
        return carry

    lax.fori_loop(0, MEMBERS * BLOCKS // CELLS, encode, 0)
    kept = pltpu.make_async_copy(coded.at[me], got_coded.at[me], local_sems.at[8 + CHUNKS])
    kept.start()

    pl.semaphore_wait(barrier, len(peers) + 2)
    for peer in peers:
        push_readings(peer)
    for chunk in range(EARLY):
        for peer in peers:
            push_prior(chunk, peer)

    def wait_all(sems, sem, ref):
        pltpu.make_async_copy(ref, ref, sems.at[sem]).wait()

    for copy in own[:-2]:
        copy.wait()
    kept.wait()

    around = 3 * BLOCKS
    tall, long = (around, CELLS), (around, MEMBERS * BLOCKS)
    which = lax.broadcasted_iota(jnp.int32, tall, 0)
    begins = jnp.zeros(tall, jnp.int32)
    for at in range(around):
        tile = lax.rem(strip + at // BLOCKS + STRIPS - 1, STRIPS) * MEMBERS + me
        begins = jnp.where(which == at, start[tile * BLOCKS + at % BLOCKS], begins)
    begins = jnp.concatenate([begins] * (MEMBERS * BLOCKS // CELLS), axis=1)
    which = lax.broadcasted_iota(jnp.int32, long, 0)
    state = lax.broadcasted_iota(jnp.int32, long, 1)
    names = ((strip + (which >> 3) - 1) * MEMBERS + me) * BLOCKS + (which & 7)
    hits = jnp.zeros(long, F32)
    for at in range(BLOCKS):
        hits = hits + jnp.where(listing[at : at + 1, :] == names, 1.0, 0.0)
    delta_x = (strip * BLOCKS + (state & 7) - begins).astype(F32)
    delta_y = ((state >> 3) - me).astype(F32)
    distance = delta_x * delta_x + delta_y * delta_y
    taper = hits * (1.0 / (1.0 + distance * (1.0 / (BLOCKS * BLOCKS)))) * (1.0 / (MEMBERS - 1))
    tile = me + (which >> 3) - 1
    tile = jnp.where(tile < 0, tile + MEMBERS, jnp.where(tile >= MEMBERS, tile - MEMBERS, tile))
    chosen = (state == tile * BLOCKS + (which & 7)).astype(F32)
    factors = lax.dot_general(
        chosen,
        taper,
        (((1,), (1,)), ((), ())),
        precision=lax.Precision.HIGHEST,
        preferred_element_type=F32,
    )
    spread_to = (around, around * MEMBERS)
    lanes = lax.broadcasted_iota(jnp.int32, spread_to, 1) >> 6
    place = (lax.broadcasted_iota(jnp.int32, spread_to, 0) == lanes).astype(F32)
    spread_out = jnp.dot(
        factors, place, precision=lax.Precision.HIGHEST, preferred_element_type=F32
    )
    for both in range(around // 2):
        pattern[:, both, :] = spread_out[:, both * CELLS : (both + 1) * CELLS]

    others = pl.ds(0, MEMBERS - 1)
    wait_all(recv_sems, 0, got_coded.at[others])
    for peer in peers:
        for chunk in range(EARLY, BEFORE):
            push_prior(chunk, peer)

    def decode(at, carry):
        group = pl.ds(at * BLOCKS, BLOCKS)
        first, second, low = (got_coded[group, word].astype(jnp.int32) for word in range(3))
        low = low + 32768
        got_model[group] = ((first << 8) + (low >> 8)).astype(F32) * (1.0 / MODEL_STEPS)
        got_noise[group] = ((second << 8) + (low & 255)).astype(F32) * (1.0 / NOISE_STEPS)
        return carry

    lax.fori_loop(0, MEMBERS // BLOCKS, decode, 0)

    slots = lax.broadcasted_iota(jnp.int32, (1, CELLS), 1)
    for block in range(BLOCKS):
        forecast = got_model[:, block, :]
        drawn = got_noise[:, block, :]
        mismatch = mine_sensor[block : block + 1, :] + drawn - forecast
        anomaly = forecast - jnp.sum(forecast, axis=0, keepdims=True) / MEMBERS
        spread = jnp.sum(anomaly * anomaly, axis=0, keepdims=True) / (MEMBERS - 1)
        active = (slots < tally[me * BLOCKS + block]).astype(F32)
        weights = mismatch * (active / (spread + mine_power[block : block + 1, :]))
        product = lax.dot_general(
            weights,
            anomaly,
            (((1,), (1,)), ((), ())),
            precision=lax.Precision.HIGHEST,
            preferred_element_type=F32,
        )
        half = (block % 2) * MEMBERS
        products[1, block // 2, :, half : half + MEMBERS] = product

    def beside_copy(slot, beside):
        return pltpu.make_async_remote_copy(
            src_ref=products.at[1],
            dst_ref=products.at[slot],
            send_sem=strip_sems.at[0, slot // 2],
            recv_sem=strip_sems.at[1, slot // 2],
            device_id=(me, beside),
            device_id_type=MESH,
        )

    copies = [beside_copy(0, east), beside_copy(2, west)]
    for copy in copies:
        copy.start()
    for copy in copies:
        copy.wait()

    low = lax.broadcasted_iota(jnp.int32, (MEMBERS, CELLS), 1) < MEMBERS

    def part_of(tile, pair):
        folded = []
        for item in range(2):
            at = tile * BLOCKS + pair * 2 + item
            total = jnp.zeros((MEMBERS, CELLS), F32)
            for both in range(around // 2):
                factor = pattern[at, both : both + 1, :]
                total = total + products[both // (BLOCKS // 2), both % (BLOCKS // 2)] * factor
            folded.append(total + pltpu.roll(total, MEMBERS, 1))
        return jnp.where(low, folded[0], folded[1])

    def fill(tile):
        def body(pair, carry):
            partial[tile, pair] = part_of(tile, pair)
            return carry

        lax.fori_loop(0, BLOCKS // 2, body, 0)

    def send_line(tile, slot, peer):
        fill(tile)
        pairs = [partial[tile, pair] for pair in range(BLOCKS // 2)]
        top = jnp.abs(pairs[0])
        for pair in pairs[1:]:
            top = jnp.maximum(top, jnp.abs(pair))
        top = jnp.max(jnp.max(top, axis=0, keepdims=True), axis=1, keepdims=True)
        top = jnp.maximum(top, 1e-30)
        factor = LINE_STEPS / top
        low_bits = jnp.full((MEMBERS, CELLS), -32768, jnp.int32)
        for at, pair in enumerate(pairs):
            code = jnp.floor(pair * factor + 0.5).astype(jnp.int32)
            line_out[slot, at] = (code >> 4).astype(jnp.int16)
            low_bits = low_bits + ((code & 15) << (4 * at))
        line_out[slot, BLOCKS // 2] = low_bits.astype(jnp.int16)
        line_unit[slot] = jnp.broadcast_to(top * (1.0 / LINE_STEPS), (BLOCKS, CELLS))
        both = [
            pltpu.make_async_remote_copy(
                src_ref=src.at[slot],
                dst_ref=dst.at[slot],
                send_sem=line_sems.at[0, at],
                recv_sem=line_sems.at[1, at],
                device_id=(peer, strip),
                device_id_type=MESH,
            )
            for at, src, dst in ((slot, line_out, line_in), (slot + 2, line_unit, got_unit))
        ]
        for copy in both:
            copy.start()
        return both

    sent = send_line(0, 0, south) + send_line(2, 1, north)
    for peer in peers:
        for chunk in range(BEFORE, CHUNKS):
            push_prior(chunk, peer)
    fill(1)
    for copy in sent:
        copy.wait()

    def line_part(slot, pair):
        shared = line_in[slot, BLOCKS // 2].astype(jnp.int32) + 32768
        code = (line_in[slot, pair].astype(jnp.int32) << 4) + ((shared >> (4 * pair)) & 15)
        return code.astype(F32) * got_unit[slot, 0:1, :]

    for pair in range(BLOCKS // 2):
        both = partial[1, pair] + line_part(0, pair) + line_part(1, pair)
        for item in range(2):
            one = both if item == 0 else pltpu.roll(both, MEMBERS, 1)
            one = one[:, 0:MEMBERS]
            one = one - jnp.sum(one, axis=1, keepdims=True) / MEMBERS
            high = one.astype(BF16)
            rest = one - high.astype(F32)
            middle = rest.astype(BF16)
            rest = rest - middle.astype(F32)
            mixing[pair * 2 + item, 0] = high
            mixing[pair * 2 + item, 1] = middle
            mixing[pair * 2 + item, 2] = rest.astype(BF16)

    def landed(chunk):
        return pltpu.make_async_copy(
            increment.at[me, pl.ds(chunk * CHUNK, CHUNK)],
            out.at[0, pl.ds(me * BLOCKS + chunk * CHUNK, CHUNK)],
            local_sems.at[8 + chunk],
        )

    for chunk in range(CHUNKS):
        wait_all(recv_sems, 2 + chunk, got_prior.at[others, pl.ds(0, CHUNK)])

        def body(step, carry):
            block = chunk * CHUNK + step
            wide_in[...] = got_prior[:, block].astype(F32).reshape(MEMBERS * LEVELS, CELLS)
            state = jnp.concatenate(
                [
                    wide_in[pl.ds(level, MEMBERS, stride=LEVELS), :].astype(BF16)
                    for level in range(LEVELS)
                ],
                axis=1,
            )
            total = jnp.zeros((MEMBERS, LEVELS * CELLS), F32)
            for term in (2, 1, 0):
                total = total + jnp.dot(mixing[block, term], state, preferred_element_type=F32)
            for level in range(LEVELS):
                wide_out[pl.ds(level, MEMBERS, stride=LEVELS), :] = total[
                    :, level * CELLS : (level + 1) * CELLS
                ]
            increment[:, block] = wide_out[...].reshape(MEMBERS, LEVELS, CELLS).astype(BF16)
            return carry

        lax.fori_loop(0, CHUNK, body, 0)
        part = pl.ds(chunk * CHUNK, CHUNK)
        landing = pl.ds(me * BLOCKS + chunk * CHUNK, CHUNK)
        for peer in peers:
            push(increment.at[peer, part], out.at[0, landing], 2 + CHUNKS + chunk, peer, strip)
        landed(chunk).start()

    for chunk in range(CHUNKS):
        landed(chunk).wait()
    wait_all(send_sems, 0, got_coded.at[others])
    one = increment.at[others, pl.ds(0, CHUNK)]
    for chunk in range(CHUNKS):
        wait_all(send_sems, 2 + chunk, one)
        wait_all(send_sems, 2 + CHUNKS + chunk, one)
        wait_all(recv_sems, 2 + CHUNKS + chunk, one)


def local(prior, model, noise, sensor, power, tally, start, listing):
    vmem, smem, anywhere = pltpu.VMEM, pltpu.SMEM, pl.ANY
    tile = (MEMBERS, BLOCKS, CELLS)
    state = (MEMBERS, BLOCKS, LEVELS, CELLS)
    packed = (BLOCKS // 2, MEMBERS, CELLS)
    dma = pltpu.SemaphoreType.DMA
    return pl.pallas_call(
        kernel,
        name="analysis",
        out_shape=vmem(prior.shape, BF16),
        in_specs=[pl.BlockSpec(memory_space=anywhere)] * 8,
        out_specs=pl.BlockSpec(memory_space=vmem),
        scratch_shapes=[
            vmem((MEMBERS * BLOCKS, CELLS), F32),
            vmem((MEMBERS * BLOCKS, CELLS), F32),
            vmem((MEMBERS, 3, BLOCKS, CELLS), jnp.int16),
            vmem((MEMBERS, 3, BLOCKS, CELLS), jnp.int16),
            vmem(tile, F32),
            vmem(tile, F32),
            vmem(state, BF16),
            vmem((BLOCKS, CELLS), F32),
            vmem((BLOCKS, CELLS), F32),
            vmem((BLOCKS, MEMBERS * BLOCKS), jnp.int32),
            smem((MEMBERS * BLOCKS,), jnp.int32),
            smem((STRIPS * MEMBERS * BLOCKS,), jnp.int32),
            vmem((3 * BLOCKS, 3 * BLOCKS // 2, CELLS), F32),
            vmem((3, *packed), F32),
            vmem((3, *packed), F32),
            vmem((2, BLOCKS // 2 + 1, MEMBERS, CELLS), jnp.int16),
            vmem((2, BLOCKS // 2 + 1, MEMBERS, CELLS), jnp.int16),
            vmem((2, BLOCKS, CELLS), F32),
            vmem((2, BLOCKS, CELLS), F32),
            vmem((BLOCKS, 3, MEMBERS, MEMBERS), BF16),
            vmem((MEMBERS * LEVELS, CELLS), F32),
            vmem((MEMBERS * LEVELS, CELLS), F32),
            vmem(state, BF16),
            dma((2 + 2 * CHUNKS,)),
            dma((2 + 2 * CHUNKS,)),
            dma((9 + CHUNKS,)),
            dma((2, 2)),
            dma((2, 4)),
        ],
        compiler_params=pltpu.CompilerParams(collective_id=0, has_side_effects=True),
    )(prior, model, noise, sensor, power, tally, start, listing.T)


def solution(mesh):
    placed = (
        P("member", "space", None, None),
        P("member", "space", None),
        P("member", "space", None),
        P("space", None),
        P("space", None),
        P("space"),
        P(),
        P("space", None),
    )
    return jax.shard_map(
        local,
        mesh=mesh,
        in_specs=placed,
        out_specs=P("member", "space", None, None),
        check_vma=False,
    )
```
